512 devices in a mesh: section: 16 (over z_hi, y, core), expert: 32 (over z_lo, x).
Axes of the slice: x: 4, y: 4, z: 16 (z_hi: 2, z_lo: 8; z = z_hi * 8 + z_lo), core: 2. Of those that a mesh axis runs over, the one named last changes fastest.
Arguments:
- tokens: bfloat16 [16, 512, 3072], P('section', 'expert'), may hold values from -6 to 6
- cotangent: bfloat16 [16, 512, 3072], P('section', 'expert'), may hold values from -0.26367188 to 0.26367188
- routes: int32 [16, 512, 2], P('section'), may hold values from 0 to 1, all different within a row
- alive: int32 [16, 2, 4], P('section'), may hold values 0 or 1
- up_half: bfloat16 [16, 2, 1536, 5376], P('section', None, None, 'expert'), may hold values from -0.109375 to 0.109375
- down_half: bfloat16 [16, 2, 5376, 1536], P('section', None, 'expert'), may hold values from -0.078125 to 0.078125
Outputs:
- up_grad: bfloat16 [16, 2, 1536, 5376], P('section', None, None, 'expert')
- down_grad: bfloat16 [16, 2, 5376, 1536], P('section', None, 'expert')
The draws below stay inside these ranges and needn't reach their ends.
Inputs may be any that keep to these rules, and one draw needn't show every extreme that they name: `routes`: in every row the two choices are different experts.
All inputs are finite; a program needn't handle non-finite values. No bound on the sum of `alive` on one device may be relied on, other than what follows from the above.
Results may differ from the reference program's by a relative error of at most 0.0054.
Values may be sent and summed in bfloat16 or wider, within the bound.
No kernel may reach another device: no remote copies, remote signals or barrier semaphores. Data moves between devices by JAX's collectives and lax.ppermute only.
A program may use at most 64 MiB of HBM per device.

```python
import jax
import jax.numpy as jnp
from jax import lax

D = 3072
FF = 5376
EXPERTS = 2
BLOCK = 128
TOKENS = 512
NBLK = 4
N_SECTION = 16


def plant(entries, rng, smallest, top_value):
    extent = entries.shape
    index_at = [jax.random.randint(jax.random.fold_in(rng, axis), (), 0, extent[axis]) for axis in range(len(extent))]
    entries = entries.at[tuple(index_at)].set(smallest)
    longest = extent.index(max(extent))
    index_at[longest] = (index_at[longest] + 1) % extent[longest]
    return entries.at[tuple(index_at)].set(top_value)


def block_scale(key, dims, cuts, low, top_value):
    loudness, own = 1.0, jax.random.fold_in(key, 6)
    for dim, parts in cuts:
        draws = jnp.exp(jax.random.uniform(jax.random.fold_in(own, dim), (parts,), jnp.float32, low / len(cuts), top_value / len(cuts)))
        loudness = loudness * jnp.repeat(draws, dims[dim] // parts).reshape([-1 if axis == dim else 1 for axis in range(len(dims))])
    return loudness


def choose_distinct(key, rows, amount, top, lift):
    sequence = jax.random.permutation(jax.random.fold_in(key, 1), amount)
    boost = sequence
    for power in range(3):
        boost = boost * boost // amount
    boost = boost * lift // amount
    tickets = jax.random.randint(jax.random.fold_in(key, 2), (rows, amount), 0, 4096) + boost
    fixed_rows = jax.random.permutation(jax.random.fold_in(key, 3), rows)[jnp.arange(amount) % rows]
    tickets = jnp.where(jnp.arange(rows)[:, None] == fixed_rows[None, :], 1 << 14, tickets)
    priority = tickets * amount + jnp.arange(amount)
    return lax.top_k(priority.astype(jnp.int32), top)[1].astype(jnp.int32)


def bell_draw(stream_key, dims, deviation, most, split=(), dtype=jnp.bfloat16):
    entries = deviation * jax.random.normal(stream_key, dims, jnp.float32)
    if split:
        entries = entries * block_scale(stream_key, dims, split, -0.22, 0.18)
    return jnp.clip(entries, -most, most).astype(dtype)


def setup_inputs(seed: int = 0) -> dict:
    keys = jax.random.split(jax.random.key(seed), 7)
    return {
        "tokens": bell_draw(keys[0], (N_SECTION, TOKENS, D), 1.0, 6.0, ((0, 16), (1, 32))),
        "cotangent": bell_draw(keys[1], (N_SECTION, TOKENS, D), (1.0 / TOKENS ** 0.5), 0.26367188, ((0, 16), (1, 32))),
        "routes": choose_distinct(keys[2], N_SECTION * TOKENS, EXPERTS, 2, 0).reshape((N_SECTION, TOKENS, 2)),
        "alive": plant((jax.random.randint(keys[3], (N_SECTION, EXPERTS, NBLK), 0, 2) < 1).astype(jnp.int32), jax.random.fold_in(keys[3], 1), 0, 1),
        "up_half": bell_draw(keys[4], (N_SECTION, EXPERTS, D // 2, FF), D ** -0.5, 0.109375, ((0, 16), (3, 32))),
        "down_half": bell_draw(keys[5], (N_SECTION, EXPERTS, FF, D // 2), FF ** -0.5, 0.078125, ((0, 16), (2, 32))),
    }


def silu_parts(pre_act):
    sigma = jax.nn.sigmoid(pre_act)
    return pre_act * sigma, sigma * (1.0 + pre_act * (1.0 - sigma))


def round_trip(values):
    rounded = lax.optimization_barrier(values.astype(jnp.bfloat16))
    return rounded.astype(jnp.float32)


def chosen_expert(route_pair, alive_rows):
    block_ids = (jnp.arange(TOKENS) // BLOCK).astype(jnp.int32)
    per_token = alive_rows[:, block_ids]
    first_pick = route_pair[:, 0]
    second_pick = route_pair[:, 1]
    alive_first = jnp.take_along_axis(per_token, first_pick[None, :], axis=0)[0]
    alive_second = jnp.take_along_axis(per_token, second_pick[None, :], axis=0)[0]
    return jnp.where(alive_first > 0, first_pick, jnp.where(alive_second > 0, second_pick, -1))


def contributions(inputs, grad_out, route_pair, alive_rows, full_up, full_down):
    chosen = chosen_expert(route_pair, alive_rows)
    up_terms = []
    down_terms = []
    for expert in range(EXPERTS):
        mask = (chosen == expert).astype(jnp.float32)[:, None]
        pre_act = jnp.dot(inputs, full_up[expert], preferred_element_type=jnp.float32)
        activated, act_slope = silu_parts(pre_act)
        hidden = (activated * mask).astype(jnp.bfloat16)
        down_terms.append(jnp.dot(hidden.T, grad_out, preferred_element_type=jnp.float32))
        back = jnp.dot(grad_out, full_down[expert].T, preferred_element_type=jnp.float32)
        dhidden = (back * act_slope * mask).astype(jnp.bfloat16)
        up_terms.append(jnp.dot(inputs.T, dhidden, preferred_element_type=jnp.float32))
    return jnp.stack(up_terms), jnp.stack(down_terms)


def reference(tokens, cotangent, routes, alive, up_half, down_half):
    half_rows = D // 2
    half_sections = N_SECTION // 2
    up_out = [None] * N_SECTION
    down_out = [None] * N_SECTION
    for low_section in range(half_sections):
        high_section = low_section + half_sections
        full_up = jnp.concatenate([up_half[low_section], up_half[high_section]], axis=1)
        full_down = jnp.concatenate([down_half[low_section], down_half[high_section]], axis=2)
        up_low, down_low = contributions(tokens[low_section], cotangent[low_section], routes[low_section], alive[low_section], full_up, full_down)
        up_high, down_high = contributions(tokens[high_section], cotangent[high_section], routes[high_section], alive[high_section], full_up, full_down)
        up_out[low_section] = (up_low[:, :half_rows] + round_trip(up_high[:, :half_rows])).astype(jnp.bfloat16)
        up_out[high_section] = (up_high[:, half_rows:] + round_trip(up_low[:, half_rows:])).astype(jnp.bfloat16)
        down_out[low_section] = (down_low[:, :, :half_rows] + round_trip(down_high[:, :, :half_rows])).astype(jnp.bfloat16)
        down_out[high_section] = (down_high[:, :, half_rows:] + round_trip(down_low[:, :, half_rows:])).astype(jnp.bfloat16)
    return jnp.stack(up_out), jnp.stack(down_out)
```

```python
import jax
import jax.numpy as jnp
from jax import lax
from jax.sharding import PartitionSpec as P

ROWS = 16
Z_SIZE = 16
X_SIZE = 4


def shift(value, dz, dx):
    pairs = []
    for section in range(16):
        for expert in range(32):
            z = (section // 8 * 8 + expert // X_SIZE + dz) % Z_SIZE
            x = (expert % X_SIZE + dx) % X_SIZE
            target = (z // 8 * 8 + section % 8, z % 8 * X_SIZE + x)
            pairs.append((section * 32 + expert, target[0] * 32 + target[1]))
    return lax.ppermute(value, ("section", "expert"), pairs)


def chosen_rows(routes, alive, expert_index):
    picks = lax.dynamic_slice_in_dim(routes, expert_index * ROWS, ROWS, 0)
    block = expert_index * ROWS // 128
    live = lax.dynamic_slice_in_dim(alive, block, 1, 1)[:, 0]
    first, second = picks[:, 0], picks[:, 1]
    alive_first = jnp.where(first == 0, live[0], live[1])
    alive_second = jnp.where(second == 0, live[0], live[1])
    return jnp.where(alive_first > 0, first, jnp.where(alive_second > 0, second, -1))


def partials(chunk, up, down, half):
    chosen = chunk[:, 2 * half].astype(jnp.float32)
    inputs, grads = chunk[:, :half], chunk[:, half : 2 * half]
    pick = chosen[None, :] > 0.5
    pre = [
        lax.dot_general(up[e], inputs, (((0,), (1,)), ((), ())), preferred_element_type=jnp.float32)
        for e in range(2)
    ]
    back = [
        lax.dot_general(down[e], grads, (((1,), (1,)), ((), ())), preferred_element_type=jnp.float32)
        for e in range(2)
    ]
    return chosen, jnp.where(pick, pre[1], pre[0]), jnp.where(pick, back[1], back[0])


def local(tokens, cotangent, routes, alive, up_half, down_half):
    half = up_half.shape[2]
    up, down = up_half[0], down_half[0]
    section, expert = lax.axis_index("section"), lax.axis_index("expert")
    z = section // 8 * 8 + expert // X_SIZE
    low = z < 8
    chosen = chosen_rows(routes[0], alive[0], expert)
    tag = jnp.broadcast_to(chosen.astype(jnp.bfloat16)[:, None], (ROWS, 128))
    tok, cot = tokens[0], cotangent[0]
    own = jnp.stack(
        [
            jnp.concatenate([tok[:, :half], cot[:, :half], tag], axis=1),
            jnp.concatenate([tok[:, half:], cot[:, half:], tag], axis=1),
        ]
    )
    from_low = shift(own, 5, 0)
    from_high = shift(own, -5, 0)
    opposite = shift(jnp.where(low, own[1], own[0]), 8, 0)
    held = [own, from_low, from_high]

    def half_for(dz):
        to_low = (z + dz) % Z_SIZE < 8
        return jnp.stack([jnp.where(to_low, b[0], b[1]) for b in held])

    block = {Z_SIZE // 2: opposite}
    for dz in (0, 1, -1, 2, -2):
        got = half_for(dz)
        got = shift(got, dz, 0) if dz else got
        for place, away in enumerate((0, -5, 5)):
            block[(away - dz) % Z_SIZE] = got[place]
    column = jnp.concatenate([block[away] for away in range(Z_SIZE)])
    left = shift(column, 0, 1)
    right = shift(column, 0, -1)
    middle = Z_SIZE * ROWS // 2
    far = [shift(left[:middle], 0, 1), shift(right[middle:], 0, -1)]
    chunks = [column, left, right, jnp.concatenate(far)]

    up_sum, down_sum = 0.0, 0.0
    for chunk in chunks:
        chosen, pre, back = partials(chunk, up, down, half)
        sent = jnp.concatenate([pre, back]).astype(jnp.bfloat16)
        sent = jnp.concatenate([sent[:, middle:], sent[:, :middle]], axis=1)
        got = shift(sent, 8, 0).astype(jnp.float32)
        width = pre.shape[0]
        pre, back = pre + got[:width], back + got[width:]
        sigma = jax.nn.sigmoid(pre)
        hidden = pre * sigma
        dhidden = back * (sigma * (1.0 + pre * (1.0 - sigma)))
        masks = [(chosen == e).astype(jnp.float32)[None, :] for e in range(2)]
        inputs, grads = chunk[:, :half], chunk[:, half : 2 * half]
        hidden = jnp.stack([(hidden * m).astype(jnp.bfloat16) for m in masks])
        dhidden = jnp.stack([(dhidden * m).astype(jnp.bfloat16) for m in masks])
        down_sum = down_sum + jnp.einsum(
            "eht,tf->ehf", hidden, grads, preferred_element_type=jnp.float32
        )
        up_sum = up_sum + jnp.einsum(
            "tf,eht->efh", inputs, dhidden, preferred_element_type=jnp.float32
        )
    return up_sum.astype(jnp.bfloat16)[None], down_sum.astype(jnp.bfloat16)[None]


def solution(mesh):
    placed = (
        P("section", "expert", None),
        P("section", "expert", None),
        P("section", None, None),
        P("section", None, None),
        P("section", None, None, "expert"),
        P("section", None, "expert", None),
    )
    return jax.shard_map(
        local,
        mesh=mesh,
        in_specs=placed,
        out_specs=(P("section", None, None, "expert"), P("section", None, "expert", None)),
        check_vma=False,
    )
```

```python
import functools

import jax
import jax.numpy as jnp
from jax import lax
from jax.experimental import pallas as pl
from jax.experimental.pallas import tpu as pltpu
from jax.sharding import PartitionSpec as P


ROWS = 16
Z_SIZE = 16
X_SIZE = 4
REACH = (1, -1, 2, -2)


def move(value, route):
    pairs = []
    for section in range(16):
        for expert in range(32):
            z, x = route(section // 8 * 8 + expert // X_SIZE, expert % X_SIZE, section % 2)
            z %= Z_SIZE
            target = (z // 8 * 8 + section % 8) * 32 + z % 8 * X_SIZE + x
            pairs.append((section * 32 + expert, target))
    return lax.ppermute(value, ("section", "expert"), pairs)


def along_z(value, step):
    return move(value, lambda z, x, core: (z + step, x))


def local_call(body, outs, scalars, *arrays, flops=0, room=8):
    vmem = pl.BlockSpec(memory_space=pltpu.VMEM)
    smem = pl.BlockSpec(memory_space=pltpu.SMEM)
    moved = sum(a.size * a.dtype.itemsize for a in (*arrays, *outs))
    return pl.pallas_call(
        body,
        out_shape=outs,
        in_specs=[smem] * len(scalars) + [vmem] * len(arrays),
        out_specs=[vmem] * len(outs),
        cost_estimate=pl.CostEstimate(flops=flops, bytes_accessed=moved, transcendentals=0),
        compiler_params=pltpu.CompilerParams(vmem_limit_bytes=room << 20),
    )(*scalars, *arrays)


def stack_kernel(tok, cot, out):
    out[0] = tok[0]
    out[1] = cot[0]


def select_kernel(z, own, low, high, mine, *sends):
    half = own.shape[2] // 2
    held = (own, low, high)

    def put(out, blocks, step):
        to_low = lax.rem(z[0] + step + Z_SIZE, Z_SIZE) < Z_SIZE // 2

        for there, cols in ((to_low, slice(0, half)), (jnp.logical_not(to_low), slice(half, None))):

            @pl.when(there)
            def _():
                for place, block in enumerate(blocks):
                    out[place] = block[:, :, cols]

    put(mine, held, 0)
    for out, step in zip(sends, REACH):
        put(out, held, step)

    @pl.when(z[1] == 0)
    def _():
        put(sends[4], (low,), 3)

    @pl.when(z[1] == 1)
    def _():
        put(sends[4], (high,), -3)


def column_kernel(mine, *refs):
    *near, last, out = refs
    places = {Z_SIZE // 2: (last, 0)}
    for source, step in zip((mine, *near), (0, *REACH)):
        for place, away in enumerate((0, -5, 5)):
            places[(away - step) % Z_SIZE] = (source, place)
    for away, (source, place) in places.items():
        out[:, away * ROWS : (away + 1) * ROWS, :] = source[place]


def product_kernel(which, chosen, up, down, rows, keep, send):
    pick = chosen[pl.ds(which[0], 1), :] > 0.5
    middle = send.shape[2] // 2
    for i, weights in enumerate((up, down)):
        first, second = (
            lax.dot_general(
                weights[e], rows[i], (((1,), (1,)), ((), ())), preferred_element_type=jnp.float32
            )
            for e in range(2)
        )
        value = jnp.where(pick, second, first)
        keep[i] = value
        value = value.astype(jnp.bfloat16)
        send[i, :, :middle] = value[:, middle:]
        send[i, :, middle:] = value[:, :middle]


def gradient_kernel(columns, last, which, chosen, *refs):
    up_out, down_out = refs[-2:]
    inputs = refs[3 * columns :][:2] if last else None
    for e in range(2):
        up_sum = inputs[0][e] if last else None
        down_sum = inputs[1][e] if last else None
        for column in range(columns):
            keep, got, rows = refs[3 * column : 3 * column + 3]
            pick = chosen[pl.ds(which[column], 1), :] == float(e)
            pre = keep[0] + got[0].astype(jnp.float32)
            back = keep[1] + got[1].astype(jnp.float32)
            sigma = jax.nn.sigmoid(pre)
            hidden = jnp.where(pick, pre * sigma, 0.0).astype(jnp.bfloat16)
            slope = sigma * (1.0 + pre * (1.0 - sigma))
            dhidden = jnp.where(pick, back * slope, 0.0).astype(jnp.bfloat16)
            more_up = jnp.dot(dhidden, rows[0], preferred_element_type=jnp.float32)
            more_down = jnp.dot(hidden, rows[1], preferred_element_type=jnp.float32)
            up_sum = more_up if up_sum is None else up_sum + more_up
            down_sum = more_down if down_sum is None else down_sum + more_down
        up_out[e] = up_sum.astype(up_out.dtype)
        down_out[e] = down_sum.astype(down_out.dtype)


def chosen_expert(routes, alive):
    tokens = routes.shape[0]
    live = jnp.broadcast_to(alive[:, :, None], (2, 4, tokens // 4)).reshape(2, tokens)
    first, second = routes[:, 0], routes[:, 1]
    alive_first = jnp.where(first == 0, live[0], live[1])
    alive_second = jnp.where(second == 0, live[0], live[1])
    return jnp.where(alive_first > 0, first, jnp.where(alive_second > 0, second, -1))


def chosen_table(mine, other, low, z):
    both = jnp.concatenate([jnp.where(low, mine, other), jnp.where(low, other, mine)])
    table = both.reshape(Z_SIZE, X_SIZE, ROWS)
    table = lax.dynamic_slice_in_dim(jnp.concatenate([table, table]), z, Z_SIZE, 0)
    return table.transpose(1, 0, 2).reshape(X_SIZE, Z_SIZE * ROWS).astype(jnp.float32)


def compute(tokens, cotangent, routes, alive, up_half, down_half):
    half, width = up_half.shape[2:]
    count = Z_SIZE * ROWS
    up = up_half[0].transpose(0, 2, 1)
    down = down_half[0]
    section, expert = lax.axis_index("section"), lax.axis_index("expert")
    z, x, core = section // 8 * 8 + expert // X_SIZE, expert % X_SIZE, section % 2

    def shape(*dims, dtype=jnp.bfloat16):
        return jax.ShapeDtypeStruct(dims, dtype)

    (own,) = local_call(stack_kernel, [shape(2, ROWS, 2 * half)], [], tokens, cotangent)
    from_low, from_high = along_z(own, 5), along_z(own, -5)
    mine = chosen_expert(routes[0], alive[0])
    other = along_z(mine.reshape(4, -1), 8).reshape(-1)
    chosen = chosen_table(mine, other, section < 8, z)
    place, chosen = lax.optimization_barrier((jnp.stack([z, core]), chosen))
    xs = jnp.stack([x, x ^ (1 + 2 * core), x ^ (3 - 2 * core), x ^ 2])

    three = shape(3, 2, ROWS, half)
    kept, *sends = local_call(
        select_kernel,
        [three] * 5 + [shape(1, 2, ROWS, half)],
        [place],
        own,
        from_low,
        from_high,
    )
    near = [along_z(v, step) for v, step in zip(sends, REACH)]
    last = move(sends[4], lambda z, x, core: (z - 3 if core else z + 3, x))
    (column,) = local_call(
        column_kernel, [shape(2, count, half)], [], kept, *near, last
    )

    def product(rows, which):
        return local_call(
            product_kernel,
            [shape(2, width, count, dtype=jnp.float32), shape(2, width, count)],
            [xs[which : which + 1]],
            chosen,
            up,
            down,
            rows,
            flops=8 * width * count * half,
            room=16,
        )

    first = move(column, lambda z, x, core: (z, x ^ (1 + 2 * core)))
    keep0, send0 = product(column, 0)
    got0 = along_z(send0, 8)
    column_again, send0 = lax.optimization_barrier((column, send0))
    second = move(column_again, lambda z, x, core: (z, x ^ (3 - 2 * core)))
    third = move(first, lambda z, x, core: (z, x ^ (3 - 2 * core)))
    keep1, send1 = product(first, 1)
    got1 = along_z(send1, 8)
    keep2, send2 = product(second, 2)
    got2 = along_z(send2, 8)
    keep3, send3 = product(third, 3)
    got3 = along_z(send3, 8)

    sums = [shape(2, width, half, dtype=jnp.float32)] * 2
    outs = [shape(2, width, half)] * 2
    keep0, _ = lax.optimization_barrier((keep0, send3))
    up_sum, down_sum = local_call(
        functools.partial(gradient_kernel, 3, False),
        sums,
        [xs[:3]],
        chosen,
        *(keep0, got0, column),
        *(keep1, got1, first),
        *(keep2, got2, second),
        flops=24 * width * count * half,
        room=28,
    )
    up_grad, down_grad = local_call(
        functools.partial(gradient_kernel, 1, True),
        outs,
        [xs[3:]],
        chosen,
        *(keep3, got3, third),
        up_sum,
        down_sum,
        flops=8 * width * count * half,
        room=20,
    )
    return up_grad.transpose(0, 2, 1)[None], down_grad[None]


def solution(mesh):
    placed = (
        P("section", "expert", None),
        P("section", "expert", None),
        P("section", None, None),
        P("section", None, None),
        P("section", None, None, "expert"),
        P("section", None, "expert", None),
    )
    return jax.shard_map(
        compute,
        mesh=mesh,
        in_specs=placed,
        out_specs=(P("section", None, None, "expert"), P("section", None, "expert", None)),
        check_vma=False,
    )
```
